32 devices in a mesh: section: 4 (over y, x), rep: 8 (over z, core).
Axes of the slice: x: 2, y: 2, z: 4, core: 2. Of those that a mesh axis runs over, the one named last changes fastest.
Arguments:
- inputs: bfloat16 [6, 256, 6144], P(None, 'rep'), may hold values from -6 to 6
- cotangent: bfloat16 [6, 256, 6144], P(None, 'rep'), may hold values from -6 to 6
- in_weight: bfloat16 [4, 6144, 256], P('section', 'rep'), may hold values from -0.078125 to 0.078125
- out_weight: bfloat16 [4, 6144, 256], P('section', 'rep'), may hold values from -0.375 to 0.375
- norm_gain: float32 [4, 6144], P('section'), may hold values from 0.5 to 1.5
- lengths: int32 [8, 6], P('rep'), may hold values from 1 to 32, 144 in all within a row
Outputs:
- grad_in_weight: bfloat16 [4, 6144, 256], P('section', 'rep')
- grad_out_weight: bfloat16 [4, 6144, 256], P('section', 'rep')
- grad_gain: float32 [4, 6144], P('section')
- grad_inputs: bfloat16 [4, 6, 256, 6144], P('section', None, 'rep')
The draws below stay inside these ranges and needn't reach their ends.
Inputs may be any that keep to these rules, and one draw needn't show every extreme that they name: `lengths`: each replica's 6 counts sum to 144 and the largest is 32.
All inputs are finite; a program needn't handle non-finite values.
Results may differ from the reference program's by a relative error of at most 0.025.
Values may be sent and summed in bfloat16 or wider, within the bound.
A program may use at most 64 MiB of HBM per device.

```python
import math
import jax
import jax.numpy as jnp
import numpy as np
from jax import lax

D = 6144
LATENT = 256
MICRO = 6
TOK_MB = 32
BATCH_ROWS = 256
ALL_ROWS = 1536
N_SECTION = 4
N_REP = 8


def block_levels(key, dims, pieces, smallest, largest):
    gain = 1.0
    for dim, parts in pieces:
        draws = jax.random.uniform(jax.random.fold_in(jax.random.fold_in(key, 6), dim), (parts,), jnp.float32, smallest / len(pieces), largest / len(pieces))
        gain = gain * jnp.repeat(jnp.exp(draws), dims[dim] // parts).reshape((-1,) + (1,) * (len(dims) - 1 - dim))
    return gain


def length_profile(amount, total, reach, skew):
    loads = [(1 << 20) // math.isqrt(grade ** skew) + 1 for grade in range(2, amount + 1)]
    rest, counts = total - reach - (amount - 1), [1] * (amount - 1)
    while rest > 0:
        free = [i for i in range(amount - 1) if counts[i] < reach]
        whole, remaining = sum([loads[i] for i in free]), rest
        for i in free:
            addition = min(reach - counts[i], max(1, remaining * loads[i] // whole), rest)
            counts[i] = counts[i] + addition
            rest = rest - addition
    return np.array([reach] + counts)


def uneven_parts(key, count, total, most, lean):
    if count == 2:
        one = jax.random.randint(key, (), max(1, total - most), min(most, total - 1) + 1)
        return jnp.stack([one, total - one])
    sizes = jnp.asarray(length_profile(count, total, most, lean), jnp.int32)
    pairs = (count - 1) // 2
    giver, receiver = sizes[1:1 + 2 * pairs:2], sizes[2:2 + 2 * pairs:2]
    slack = jnp.minimum(giver - 1, most - receiver)
    passed = jax.random.randint(jax.random.fold_in(key, 1), (pairs,), 0, 1 << 20) % (slack + 1)
    sizes = sizes.at[1:1 + 2 * pairs:2].set(giver - passed).at[2:2 + 2 * pairs:2].set(receiver + passed)
    return sizes[jax.random.permutation(jax.random.fold_in(key, 2), count)]


def normal_values(stream_key, dims, deviation, limit, shards=(), kind=jnp.bfloat16):
    result = jax.random.normal(stream_key, dims, jnp.float32) * deviation
    if len(shards) > 0:
        result = block_levels(stream_key, dims, shards, -0.22, 0.18) * result
    return jnp.clip(result, min=-limit, max=limit).astype(kind)


def setup_inputs(seed: int = 0) -> dict:
    splits = jax.random.split(jax.random.key(seed), 7)
    return {
        "inputs": normal_values(splits[0], (MICRO, BATCH_ROWS, D), 1.0, 6.0, ((1, 8),)),
        "cotangent": normal_values(splits[1], (MICRO, BATCH_ROWS, D), 1.0, 6.0, ((1, 8),)),
        "in_weight": normal_values(splits[2], (N_SECTION, D, LATENT), D ** -0.5, 0.078125, ((0, 4), (1, 8))),
        "out_weight": normal_values(splits[3], (N_SECTION, D, LATENT), LATENT ** -0.5, 0.375, ((0, 4), (1, 8))),
        "norm_gain": jnp.clip(1.0 + 0.1 * jax.random.normal(splits[4], (N_SECTION, D), jnp.float32), 0.5, 1.5),
        "lengths": jax.vmap(lambda own: uneven_parts(own, MICRO, MICRO * TOK_MB * 3 // 4, TOK_MB, 2))(jax.random.split(splits[5], N_REP)).reshape((N_REP, MICRO)).astype(jnp.int32),
    }


norm_epsilon = 1e-05

def section_forward(hidden, norm_gain, in_weight, out_weight):
    widened = hidden.astype(jnp.float32)
    inverse = lax.rsqrt(lax.optimization_barrier(jnp.mean(widened * widened, axis=-1, keepdims=True)) + norm_epsilon)
    normed = (widened * inverse * norm_gain).astype(jnp.bfloat16)
    before = jnp.dot(normed, in_weight, preferred_element_type=jnp.float32)
    activated = jax.nn.silu(before).astype(jnp.bfloat16)
    mixed = lax.dot_general(activated, out_weight, (((1,), (1,)), ((), ())), preferred_element_type=jnp.float32)
    return ((widened + mixed).astype(jnp.bfloat16), normed, before, activated)

def section_backward(hidden, norm_gain, in_weight, out_weight, before, upstream):
    widened = hidden.astype(jnp.float32)
    inverse = lax.rsqrt(lax.optimization_barrier(jnp.mean(widened * widened, axis=-1, keepdims=True)) + norm_epsilon)
    grad_activated = jnp.dot(upstream, out_weight, preferred_element_type=jnp.float32)
    sigmoid_value = jax.nn.sigmoid(before)
    grad_before = (grad_activated * sigmoid_value * (1.0 + before * (1.0 - sigmoid_value))).astype(jnp.bfloat16)
    grad_normed = lax.dot_general(grad_before, in_weight, (((1,), (1,)), ((), ())), preferred_element_type=jnp.float32)
    grad_scaled = grad_normed * norm_gain
    projection = lax.optimization_barrier(jnp.mean(grad_scaled * widened, axis=-1, keepdims=True))
    grad_hidden = upstream.astype(jnp.float32) + inverse * grad_scaled - widened * (inverse * inverse * inverse) * projection
    gain_terms = lax.optimization_barrier(jnp.sum(grad_normed * widened * inverse, axis=0))
    return (grad_hidden.astype(jnp.bfloat16), grad_before, gain_terms)

def replica_sum(left, right, grad_scale):
    left_parts = left.reshape(MICRO, N_REP, TOK_MB, left.shape[-1])
    right_parts = right.reshape(MICRO, N_REP, TOK_MB, right.shape[-1])

    def add_one(total, replica):
        left_rows = lax.dynamic_index_in_dim(left_parts, replica, 1, keepdims=False).reshape(MICRO * TOK_MB, left.shape[-1])
        right_rows = lax.dynamic_index_in_dim(right_parts, replica, 1, keepdims=False).reshape(MICRO * TOK_MB, right.shape[-1])
        term = lax.dot_general(left_rows, right_rows, (((0,), (0,)), ((), ())), preferred_element_type=jnp.float32) * grad_scale
        rounded = lax.optimization_barrier(term.astype(jnp.bfloat16)).astype(jnp.float32)
        return (total + rounded, None)
    start_total = jnp.zeros((left.shape[-1], right.shape[-1]), jnp.float32)
    total, unused = lax.scan(add_one, start_total, jnp.arange(N_REP, dtype=jnp.int32))
    return total.astype(jnp.bfloat16)

def reference(inputs, cotangent, in_weight, out_weight, norm_gain, lengths):
    row_total = MICRO * BATCH_ROWS
    grad_scale = 1.0 / math.sqrt(ALL_ROWS)
    hidden = inputs.reshape(row_total, D)
    saved = []
    for section_index in range(N_SECTION):
        leaving, normed, before, activated = section_forward(hidden, norm_gain[section_index], in_weight[section_index], out_weight[section_index])
        saved.append((hidden, normed, before, activated))
        hidden = leaving
    position = jnp.arange(TOK_MB, dtype=jnp.int32)
    keep_rows = position[None, None, :] < jnp.transpose(lengths)[:, :, None]
    upstream = jnp.where(keep_rows.reshape(row_total, 1), cotangent.reshape(row_total, D), jnp.zeros((), jnp.bfloat16))
    grads_in = [None] * N_SECTION
    grads_out = [None] * N_SECTION
    grads_gain = [None] * N_SECTION
    grads_hidden = [None] * N_SECTION
    for section_index in reversed(range(N_SECTION)):
        hidden, normed, before, activated = saved[section_index]
        grad_hidden, grad_before, gain_terms = section_backward(hidden, norm_gain[section_index], in_weight[section_index], out_weight[section_index], before, upstream)
        grads_in[section_index] = replica_sum(normed, grad_before, grad_scale)
        grads_out[section_index] = replica_sum(upstream, activated, grad_scale)
        grads_gain[section_index] = gain_terms * grad_scale
        grads_hidden[section_index] = grad_hidden.reshape(MICRO, BATCH_ROWS, D)
        upstream = grad_hidden
    return (jnp.stack(grads_in), jnp.stack(grads_out), jnp.stack(grads_gain), jnp.stack(grads_hidden))
```

```python
import functools
import math

import jax
import jax.numpy as jnp
from jax import lax
from jax.experimental import pallas as pl
from jax.experimental.pallas import tpu as pltpu
from jax.sharding import PartitionSpec as P

norm_epsilon = 1e-05


def from_behind(block, axis, distance):
    devices = range(lax.axis_size(axis))
    route = [(i - distance, i) for i in devices if i - distance in devices]
    return lax.ppermute(block, axis, route)


def section_forward(hidden, norm_gain, in_weight, out_weight):
    widened = hidden.astype(jnp.float32)
    inverse = lax.rsqrt(jnp.mean(widened * widened, axis=-1, keepdims=True) + norm_epsilon)
    normed = (widened * inverse * norm_gain).astype(jnp.bfloat16)
    before = jnp.dot(normed, in_weight, preferred_element_type=jnp.float32)
    activated = jax.nn.silu(before).astype(jnp.bfloat16)
    mixed = lax.dot_general(
        activated, out_weight, (((1,), (1,)), ((), ())), preferred_element_type=jnp.float32
    )
    return ((widened + mixed).astype(jnp.bfloat16), normed, before, activated)


def section_backward(hidden, norm_gain, in_weight, out_weight, before, upstream):
    widened = hidden.astype(jnp.float32)
    inverse = lax.rsqrt(jnp.mean(widened * widened, axis=-1, keepdims=True) + norm_epsilon)
    grad_activated = jnp.dot(upstream, out_weight, preferred_element_type=jnp.float32)
    sigmoid_value = jax.nn.sigmoid(before)
    grad_before = (grad_activated * sigmoid_value * (1.0 + before * (1.0 - sigmoid_value))).astype(
        jnp.bfloat16
    )
    grad_normed = lax.dot_general(
        grad_before, in_weight, (((1,), (1,)), ((), ())), preferred_element_type=jnp.float32
    )
    grad_scaled = grad_normed * norm_gain
    projection = jnp.mean(grad_scaled * widened, axis=-1, keepdims=True)
    grad_hidden = (
        upstream.astype(jnp.float32)
        + inverse * grad_scaled
        - widened * (inverse * inverse * inverse) * projection
    )
    gain_terms = jnp.sum(grad_normed * widened * inverse, axis=0)
    return (grad_hidden.astype(jnp.bfloat16), grad_before, gain_terms)


def write_slot(holders, contents, slot):
    return tuple(
        (
            lax.dynamic_update_index_in_dim(holder, content, slot, 0)
            for holder, content in zip(holders, contents)
        )
    )


def staged_body(inputs, cotangent, in_weight, out_weight, norm_gain, lengths):
    section_count = lax.axis_size("section")
    replicas = lax.axis_size("rep")
    position = lax.axis_index("section")
    micro_count, tok_rows, width = inputs.shape
    grad_scale = 1.0 / math.sqrt(micro_count * tok_rows * replicas)
    gain_row = norm_gain[0]
    full_in, full_out = (
        lax.all_gather(in_weight[0], "rep", axis=0, tiled=True),
        lax.all_gather(out_weight[0], "rep", axis=0, tiled=True),
    )
    rank_width = full_in.shape[1]
    tick_total = micro_count + section_count - 1
    blank = jnp.zeros((tok_rows, width), jnp.bfloat16)
    wide_zeros = jnp.zeros((micro_count, tok_rows, width), jnp.bfloat16)
    narrow_zeros = jnp.zeros((micro_count, tok_rows, rank_width), jnp.bfloat16)
    stores = (wide_zeros,)

    def forward_tick(moment, carried):
        received, holders = carried
        micro = moment - position
        active = (micro >= 0) & (micro < micro_count)
        slot = jnp.clip(micro, 0, micro_count - 1)
        fresh = lax.dynamic_index_in_dim(inputs, slot, 0, keepdims=False)
        entering = jnp.where(position == 0, fresh, received)

        def forward_run_section(holders):
            leaving, normed, before, activated = section_forward(
                entering, gain_row, full_in, full_out
            )
            contents = (entering,)
            return (leaving, write_slot(holders, contents, slot))

        def forward_skip_section(holders):
            return (blank, holders)

        leaving, holders = lax.cond(active, forward_run_section, forward_skip_section, holders)
        received = from_behind(leaving, "section", 1)
        return (received, holders)

    received, stores = lax.fori_loop(0, tick_total, forward_tick, (blank, stores))
    keep_rows = jnp.arange(tok_rows, dtype=jnp.int32)[None, :] < lengths[0][:, None]
    seeds = jnp.where(keep_rows[:, :, None], cotangent, jnp.zeros((), jnp.bfloat16))
    gain_start = jnp.zeros((width,), jnp.float32)
    buffers = (wide_zeros, narrow_zeros, wide_zeros, wide_zeros, narrow_zeros)

    def backward_tick(moment, carried):
        received, holders, gain_total = carried
        micro = moment - (section_count - 1 - position)
        active = (micro >= 0) & (micro < micro_count)
        slot = jnp.clip(micro, 0, micro_count - 1)
        seed_rows = lax.dynamic_index_in_dim(seeds, slot, 0, keepdims=False)
        entering = jnp.where(position == section_count - 1, seed_rows, received)

        def backward_run_section(operands):
            holders, gain_total = operands
            hidden_rows = lax.dynamic_index_in_dim(stores[0], slot, 0, keepdims=False)
            unused, normed, before, activated = section_forward(
                hidden_rows, gain_row, full_in, full_out
            )
            grad_hidden, grad_before, gain_terms = section_backward(
                hidden_rows, gain_row, full_in, full_out, before, entering
            )
            contents = (grad_hidden, grad_before, entering, normed, activated)
            return (grad_hidden, (write_slot(holders, contents, slot), gain_total + gain_terms))

        def backward_skip_section(operands):
            return (blank, operands)

        leaving, (holders, gain_total) = lax.cond(
            active, backward_run_section, backward_skip_section, (holders, gain_total)
        )
        received = from_behind(leaving, "section", -1)
        return (received, holders, gain_total)

    received, buffers, gain_total = lax.fori_loop(
        0, tick_total, backward_tick, (blank, buffers, gain_start)
    )
    normed_all = buffers[3]
    activated_all = buffers[4]
    flat_rows = micro_count * tok_rows
    normed_flat = normed_all.reshape(flat_rows, width)
    upstream_flat = buffers[2].reshape(flat_rows, width)
    before_flat = buffers[1].reshape(flat_rows, rank_width)
    activated_flat = activated_all.reshape(flat_rows, rank_width)
    left_term = lax.dot_general(
        normed_flat, before_flat, (((0,), (0,)), ((), ())), preferred_element_type=jnp.float32
    )
    right_term = lax.dot_general(
        upstream_flat, activated_flat, (((0,), (0,)), ((), ())), preferred_element_type=jnp.float32
    )
    summed = lax.psum_scatter(
        (jnp.concatenate((left_term, right_term), axis=1) * grad_scale).astype(jnp.bfloat16),
        "rep",
        scatter_dimension=0,
        tiled=True,
    ).astype(jnp.float32)
    grad_in_weight = summed[:, :rank_width].astype(jnp.bfloat16)[None]
    grad_out_weight = summed[:, rank_width:].astype(jnp.bfloat16)[None]
    grad_gain = lax.psum(gain_total * grad_scale, "rep")[None]
    grad_inputs = buffers[0][None]
    return (grad_in_weight, grad_out_weight, grad_gain, grad_inputs)


MESH = pl.DeviceIdType.MESH
contract_last = (((1,), (1,)), ((), ()))
contract_rows = (((0,), (0,)), ((), ()))
carrier = 128


def two_halves(column):
    high = column.astype(jnp.bfloat16).astype(jnp.float32)
    low = column - high
    lane = lax.broadcasted_iota(jnp.int32, (column.shape[0], carrier), 1)
    return jnp.where(lane == 0, high, jnp.where(lane == 1, low, 0.0)).astype(jnp.bfloat16)


def window_kernel(
    sections, replicas, grad_scale,
    x_ref, c_ref, wg_ref, wo_ref, raw_ref, gain_ref,
    gin_ref, gout_ref, gain_out_ref, rows_out_ref,
    hid, up, wgb, wob, fs_out, fs_in, bs_out, bs_in, act, gbi, before, inverse,
    m_out, n_out, m_in, n_in, gain_own,
    x_send, x_recv, c_send, c_recv, wg_send, wg_recv, wo_send, wo_recv,
    fs_send, fs_recv, fg_send, fg_recv, bs_send, bs_recv, bg_send, bg_recv,
    m_send, m_recv, n_send, n_recv, r_send, r_recv, own_sem, g_send, g_recv,
):
    chunk, block = x_ref.shape[1], x_ref.shape[2]
    rank = wg_ref.shape[1]
    width = block * replicas
    sec, rep = lax.axis_index("section"), lax.axis_index("rep")

    def place(r):
        return pl.ds(pl.multiple_of(r * chunk, 16), chunk)

    def lanes(r):
        return pl.ds(pl.multiple_of(r * block, 128), block)

    def to_rep(src, dst, send, recv, peer):
        return pltpu.make_async_remote_copy(
            src_ref=src, dst_ref=dst, send_sem=send, recv_sem=recv,
            device_id={"section": sec, "rep": peer}, device_id_type=MESH,
        )

    def to_sec(src, dst, send, recv, peer):
        return pltpu.make_async_remote_copy(
            src_ref=src, dst_ref=dst, send_sem=send, recv_sem=recv,
            device_id={"section": peer, "rep": rep}, device_id_type=MESH,
        )

    def each_rep(step):
        def go(i, carry):
            step(lax.rem(rep + i, replicas))
            return carry
        lax.fori_loop(1, replicas, go, 0)

    def each_sec(step):
        def go(i, carry):
            step(lax.rem(sec + i, sections))
            return carry
        lax.fori_loop(1, sections, go, 0)

    barrier = pltpu.get_barrier_semaphore()
    count = sections * replicas
    mine = sec * replicas + rep

    def greet(i, carry):
        other = lax.rem(mine + i, count)
        pl.semaphore_signal(
            barrier, inc=1,
            device_id={"section": other // replicas, "rep": lax.rem(other, replicas)},
            device_id_type=MESH,
        )
        return carry

    lax.fori_loop(1, count, greet, 0)
    pl.semaphore_wait(barrier, count - 1)

    def x_copy(peer, source):
        return to_rep(x_ref.at[peer], hid.at[0, place(source)], x_send.at[peer], x_recv.at[source], peer)

    def c_copy(peer, source):
        return to_rep(
            c_ref.at[peer], up.at[sections, place(source)], c_send.at[peer], c_recv.at[source], peer
        )

    def wg_copy(peer, source):
        return to_sec(wg_ref, wgb.at[source], wg_send.at[peer], wg_recv.at[source], peer)

    def wo_copy(peer, source):
        return to_sec(wo_ref, wob.at[source], wo_send.at[peer], wo_recv.at[source], peer)

    each_rep(lambda peer: x_copy(peer, rep).start())
    each_sec(lambda peer: wg_copy(peer, sec).start())
    each_sec(lambda peer: wo_copy(peer, sec).start())
    hid[0, place(rep)] = x_ref[rep]
    up[sections, place(rep)] = c_ref[rep]
    wgb[sec] = wg_ref[...]
    wob[sec] = wo_ref[...]
    each_rep(lambda peer: x_copy(peer, peer).wait_recv())
    each_rep(lambda peer: c_copy(peer, rep).start())

    def fs_copy(s, peer, source):
        return to_rep(
            fs_out.at[s, place(peer)], fs_in.at[s, source], fs_send.at[s, peer], fs_recv.at[s, source], peer
        )

    def bs_copy(s, peer, source):
        return to_rep(
            bs_out.at[s, place(peer)], bs_in.at[s, source], bs_send.at[s, peer], bs_recv.at[s, source], peer
        )

    def fg_copy(s, peer, source):
        view = act.at[s, place(source)]
        return to_rep(view, view, fg_send.at[s, peer], fg_recv.at[s, source], peer)

    def bg_copy(s, peer, source):
        view = gbi.at[s, place(source)]
        return to_rep(view, view, bg_send.at[s, peer], bg_recv.at[s, source], peer)

    def m_copy(s, source):
        return to_sec(m_out.at[s], m_in.at[source], m_send.at[s], m_recv.at[source], s)

    def n_copy(s, source):
        return to_sec(n_out.at[s], n_in.at[source], n_send.at[s], n_recv.at[source], s)

    def forward_send(s):
        @pl.when(s != sec)
        def _():
            wg_copy(s, s).wait_recv()

        hidden = hid[s]
        partial = jnp.dot(hidden, wgb[s], preferred_element_type=jnp.float32)
        fs_out[s, :, pl.ds(0, rank)] = partial.astype(jnp.bfloat16)
        widened = hidden.astype(jnp.float32)
        fs_out[s, :, pl.ds(rank, carrier)] = two_halves(jnp.sum(widened * widened, axis=1, keepdims=True))
        each_rep(lambda peer: fs_copy(s, peer, rep).start())

    def summed(copy, out, landing, s):
        def go(i, total):
            source = lax.rem(rep + i, replicas)
            copy(s, source, source).wait_recv()
            return total + landing[s, source].astype(jnp.float32)
        return lax.fori_loop(1, replicas, go, out[s, place(rep)].astype(jnp.float32))

    def forward_finish(s):
        total = summed(fs_copy, fs_out, fs_in, s)
        square = total[:, rank:rank + 1] + total[:, rank + 1:rank + 2]
        inv = lax.rsqrt(square / width + norm_epsilon)
        value = total[:, :rank] * inv
        before[s] = value
        inverse[s] = jnp.broadcast_to(inv, (chunk, carrier))
        act[s, place(rep)] = (value / (1.0 + jnp.exp(-value))).astype(jnp.bfloat16)
        each_rep(lambda peer: fg_copy(s, peer, rep).start())

    def wait_act(s):
        each_rep(lambda peer: fg_copy(s, peer, peer).wait_recv())

    def wait_wo(s):
        @pl.when(s != sec)
        def _():
            wo_copy(s, s).wait_recv()

    def backward_send(s):
        bs_out[s] = jnp.dot(up[s + 1], wob[s], preferred_element_type=jnp.float32).astype(jnp.bfloat16)
        each_rep(lambda peer: bs_copy(s, peer, rep).start())

    def backward_finish(s):
        grad_activated = summed(bs_copy, bs_out, bs_in, s)
        value = before[s]
        inv = inverse[s][:, :1]
        sig = 1.0 / (1.0 + jnp.exp(-value))
        grad_before = grad_activated * sig * (1.0 + value * (1.0 - sig))
        share = inv * inv * jnp.sum(grad_before * value, axis=1, keepdims=True) / width
        gbi[s, place(rep), pl.ds(0, rank)] = (grad_before * inv).astype(jnp.bfloat16)
        gbi[s, place(rep), pl.ds(rank, carrier)] = two_halves(share)
        each_rep(lambda peer: bg_copy(s, peer, rep).start())

    def upstream_step(s):
        each_rep(lambda peer: bg_copy(s, peer, peer).wait_recv())
        grads = gbi[s]
        tail = grads[:, rank:].astype(jnp.float32)
        share = tail[:, 0:1] + tail[:, 1:2]
        spread = lax.dot_general(grads[:, :rank], wgb[s], contract_last, preferred_element_type=jnp.float32)
        up[s] = (
            up[s + 1].astype(jnp.float32) + spread - hid[s].astype(jnp.float32) * share
        ).astype(jnp.bfloat16)

    def rows_copy(s, r, from_s, from_r):
        return pltpu.make_async_remote_copy(
            src_ref=up.at[s, place(r)],
            dst_ref=rows_out_ref.at[place(from_s), lanes(from_r)],
            send_sem=r_send.at[s, r], recv_sem=r_recv.at[from_s, from_r],
            device_id={"section": s, "rep": r}, device_id_type=MESH,
        )

    def own_rows():
        return pltpu.make_async_copy(
            up.at[sec, place(rep)], rows_out_ref.at[place(sec), lanes(rep)], own_sem
        )

    def send_rows(s):
        each_rep(lambda r: rows_copy(s, r, sec, rep).start())

        @pl.when(s == sec)
        def _():
            own_rows().start()

        @pl.when(s != sec)
        def _():
            rows_copy(s, rep, sec, rep).start()

    def m_step(s):
        m_out[s] = lax.dot_general(
            hid[s], gbi[s, :, pl.ds(0, rank)], contract_rows, preferred_element_type=jnp.float32
        ).astype(jnp.bfloat16)

        @pl.when(s != sec)
        def _():
            m_copy(s, sec).start()

    def n_step(s):
        n_out[s] = lax.dot_general(
            up[s + 1], act[s], contract_rows, preferred_element_type=jnp.float32
        ).astype(jnp.bfloat16)

        @pl.when(s != sec)
        def _():
            n_copy(s, sec).start()

    def forward(s, carry):
        forward_send(s)
        forward_finish(s)
        wait_wo(s)
        wait_act(s)
        mixed = lax.dot_general(act[s], wob[s], contract_last, preferred_element_type=jnp.float32)
        hid[s + 1] = (hid[s].astype(jnp.float32) + mixed).astype(jnp.bfloat16)
        return carry

    lax.fori_loop(0, sections - 1, forward, 0)
    last = sections - 1
    forward_send(last)
    wait_wo(last)
    each_rep(lambda peer: c_copy(peer, peer).wait_recv())
    backward_send(last)
    forward_finish(last)
    backward_finish(last)
    wait_act(last)
    n_step(last)
    upstream_step(last)

    def backward(i, carry):
        s = last - i
        backward_send(s)
        send_rows(s + 1)
        m_step(s + 1)
        n_step(s)
        backward_finish(s)
        upstream_step(s)
        return carry

    lax.fori_loop(1, sections, backward, 0)
    m_step(0)
    send_rows(0)

    each_sec(lambda peer: n_copy(sec, peer).wait_recv())

    def add_parts(own, landing):
        total = own[sec].astype(jnp.float32)
        for i in range(1, sections):
            total = total + landing[lax.rem(sec + i, sections)].astype(jnp.float32)
        return total * grad_scale

    gout_ref[...] = add_parts(n_out, n_in).astype(jnp.bfloat16)
    each_sec(lambda peer: m_copy(sec, peer).wait_recv())
    product = add_parts(m_out, m_in)
    gin_ref[...] = (product * gain_ref[...]).astype(jnp.bfloat16)
    terms = product * raw_ref[...].astype(jnp.float32)
    high = terms.astype(jnp.bfloat16)
    low = (terms - high.astype(jnp.float32)).astype(jnp.bfloat16)
    ones = jnp.ones((8, rank), jnp.bfloat16)
    gain_own[...] = lax.dot_general(
        ones, high, contract_last, preferred_element_type=jnp.float32
    ) + lax.dot_general(ones, low, contract_last, preferred_element_type=jnp.float32)

    def g_copy(peer, source):
        return to_rep(
            gain_own, gain_out_ref.at[:, lanes(source)], g_send.at[peer], g_recv.at[source], peer
        )

    each_rep(lambda peer: g_copy(peer, rep).start())
    gain_out_ref[:, lanes(rep)] = gain_own[...]

    def each_section(step):
        def go(s, carry):
            step(s)
            return carry
        lax.fori_loop(0, sections, go, 0)

    def sent(s):
        each_rep(lambda peer: fs_copy(s, peer, rep).wait_send())
        each_rep(lambda peer: fg_copy(s, peer, rep).wait_send())
        each_rep(lambda peer: bs_copy(s, peer, rep).wait_send())
        each_rep(lambda peer: bg_copy(s, peer, rep).wait_send())
        each_rep(lambda peer: rows_copy(s, peer, sec, rep).wait_send())
        each_rep(lambda peer: rows_copy(sec, peer, s, peer).wait_recv())

        @pl.when(s != sec)
        def _():
            rows_copy(s, rep, sec, rep).wait_send()
            rows_copy(s, rep, s, rep).wait_recv()
            wg_copy(s, sec).wait_send()
            wo_copy(s, sec).wait_send()
            m_copy(s, sec).wait_send()
            n_copy(s, sec).wait_send()

    each_section(sent)
    own_rows().wait()
    each_rep(lambda peer: x_copy(peer, rep).wait_send())
    each_rep(lambda peer: c_copy(peer, rep).wait_send())
    each_rep(lambda peer: g_copy(peer, rep).wait_send())
    each_rep(lambda peer: g_copy(peer, peer).wait_recv())


def window_body(inputs, cotangent, in_weight, out_weight, norm_gain, lengths):
    sections, replicas = lax.axis_size("section"), lax.axis_size("rep")
    sec, rep = lax.axis_index("section"), lax.axis_index("rep")
    micro_count, tok_rows, width = inputs.shape
    block, rank = in_weight.shape[1:]
    own_rows = micro_count * tok_rows
    chunk = own_rows // sections
    rows = chunk * replicas
    grad_scale = 1.0 / math.sqrt(own_rows * replicas)
    keep = jnp.arange(tok_rows, dtype=jnp.int32)[None, :] < lengths[0][:, None]

    def part(array):
        piece = lax.dynamic_slice_in_dim(array.reshape(own_rows, width), sec * chunk, chunk, 0)
        return piece.reshape(chunk, replicas, block).transpose(1, 0, 2)

    kept = lax.dynamic_slice_in_dim(keep.reshape(own_rows), sec * chunk, chunk, 0)
    x_parts = part(inputs)
    c_parts = jnp.where(kept[None, :, None], part(cotangent), jnp.zeros((), jnp.bfloat16))
    gain = lax.dynamic_slice_in_dim(norm_gain[0], rep * block, block, 0)[:, None]
    scaled = (in_weight[0].astype(jnp.float32) * gain).astype(jnp.bfloat16)
    bf, f32 = jnp.bfloat16, jnp.float32
    dma = pltpu.SemaphoreType.DMA
    vmem = pl.BlockSpec(memory_space=pltpu.VMEM)
    wide = rank + carrier
    grad_in, grad_out, grad_gain, grad_rows = pl.pallas_call(
        functools.partial(window_kernel, sections, replicas, grad_scale),
        out_shape=(
            jax.ShapeDtypeStruct((block, rank), bf),
            jax.ShapeDtypeStruct((block, rank), bf),
            jax.ShapeDtypeStruct((8, width), f32),
            jax.ShapeDtypeStruct((own_rows, width), bf),
        ),
        in_specs=[vmem] * 6,
        out_specs=(vmem, vmem, vmem, pl.BlockSpec(memory_space=pl.ANY)),
        scratch_shapes=[
            pltpu.VMEM((sections, rows, block), bf),
            pltpu.VMEM((sections + 1, rows, block), bf),
            pltpu.VMEM((sections, block, rank), bf),
            pltpu.VMEM((sections, block, rank), bf),
            pltpu.VMEM((sections, rows, wide), bf),
            pltpu.VMEM((sections, replicas, chunk, wide), bf),
            pltpu.VMEM((sections, rows, rank), bf),
            pltpu.VMEM((sections, replicas, chunk, rank), bf),
            pltpu.VMEM((sections, rows, rank), bf),
            pltpu.VMEM((sections, rows, wide), bf),
            pltpu.VMEM((sections, chunk, rank), f32),
            pltpu.VMEM((sections, chunk, carrier), f32),
            pltpu.VMEM((sections, block, rank), bf),
            pltpu.VMEM((sections, block, rank), bf),
            pltpu.VMEM((sections, block, rank), bf),
            pltpu.VMEM((sections, block, rank), bf),
            pltpu.VMEM((8, block), f32),
            *[dma((replicas,))] * 4,
            *[dma((sections,))] * 4,
            *[dma((sections, replicas))] * 8,
            *[dma((sections,))] * 4,
            *[dma((sections, replicas))] * 2,
            dma,
            *[dma((replicas,))] * 2,
        ],
        compiler_params=pltpu.CompilerParams(
            collective_id=0, has_side_effects=True, vmem_limit_bytes=60 * 1024 * 1024
        ),
        name="adapter_window",
    )(x_parts, c_parts, scaled, out_weight[0], in_weight[0], gain)
    return (
        grad_in[None],
        grad_out[None],
        grad_gain[:1],
        grad_rows.reshape(1, micro_count, tok_rows, width),
    )


def body(inputs, cotangent, in_weight, out_weight, norm_gain, lengths):
    sections = lax.axis_size("section")
    block, rank = in_weight.shape[1:]
    own_rows = inputs.shape[0] * inputs.shape[1]
    aligned = own_rows % (16 * sections) == 0 and block % 128 == 0 and rank % 128 == 0
    chosen = window_body if aligned else staged_body
    return chosen(inputs, cotangent, in_weight, out_weight, norm_gain, lengths)


def solution(mesh):
    in_specs = (
        P(None, "rep", None),
        P(None, "rep", None),
        P("section", "rep", None),
        P("section", "rep", None),
        P("section", None),
        P("rep", None),
    )
    out_specs = (
        P("section", "rep", None),
        P("section", "rep", None),
        P("section", None),
        P("section", None, "rep", None),
    )
    return jax.shard_map(body, mesh=mesh, in_specs=in_specs, out_specs=out_specs, check_vma=False)
```

```python
import functools
import math

import jax
import jax.numpy as jnp
from jax import lax
from jax.experimental import pallas as pl
from jax.experimental.pallas import tpu as pltpu
from jax.sharding import PartitionSpec as P

norm_epsilon = 1e-05


def from_behind(block, axis, distance):
    devices = range(lax.axis_size(axis))
    route = [(i - distance, i) for i in devices if i - distance in devices]
    return lax.ppermute(block, axis, route)


def section_forward(hidden, norm_gain, in_weight, out_weight):
    widened = hidden.astype(jnp.float32)
    inverse = lax.rsqrt(jnp.mean(widened * widened, axis=-1, keepdims=True) + norm_epsilon)
    normed = (widened * inverse * norm_gain).astype(jnp.bfloat16)
    before = jnp.dot(normed, in_weight, preferred_element_type=jnp.float32)
    activated = jax.nn.silu(before).astype(jnp.bfloat16)
    mixed = lax.dot_general(
        activated, out_weight, (((1,), (1,)), ((), ())), preferred_element_type=jnp.float32
    )
    return ((widened + mixed).astype(jnp.bfloat16), normed, before, activated)


def section_backward(hidden, norm_gain, in_weight, out_weight, before, upstream):
    widened = hidden.astype(jnp.float32)
    inverse = lax.rsqrt(jnp.mean(widened * widened, axis=-1, keepdims=True) + norm_epsilon)
    grad_activated = jnp.dot(upstream, out_weight, preferred_element_type=jnp.float32)
    sigmoid_value = jax.nn.sigmoid(before)
    grad_before = (grad_activated * sigmoid_value * (1.0 + before * (1.0 - sigmoid_value))).astype(
        jnp.bfloat16
    )
    grad_normed = lax.dot_general(
        grad_before, in_weight, (((1,), (1,)), ((), ())), preferred_element_type=jnp.float32
    )
    grad_scaled = grad_normed * norm_gain
    projection = jnp.mean(grad_scaled * widened, axis=-1, keepdims=True)
    grad_hidden = (
        upstream.astype(jnp.float32)
        + inverse * grad_scaled
        - widened * (inverse * inverse * inverse) * projection
    )
    gain_terms = jnp.sum(grad_normed * widened * inverse, axis=0)
    return (grad_hidden.astype(jnp.bfloat16), grad_before, gain_terms)


def write_slot(holders, contents, slot):
    return tuple(
        (
            lax.dynamic_update_index_in_dim(holder, content, slot, 0)
            for holder, content in zip(holders, contents)
        )
    )


def staged_body(inputs, cotangent, in_weight, out_weight, norm_gain, lengths):
    section_count = lax.axis_size("section")
    replicas = lax.axis_size("rep")
    position = lax.axis_index("section")
    micro_count, tok_rows, width = inputs.shape
    grad_scale = 1.0 / math.sqrt(micro_count * tok_rows * replicas)
    gain_row = norm_gain[0]
    full_in, full_out = (
        lax.all_gather(in_weight[0], "rep", axis=0, tiled=True),
        lax.all_gather(out_weight[0], "rep", axis=0, tiled=True),
    )
    rank_width = full_in.shape[1]
    tick_total = micro_count + section_count - 1
    blank = jnp.zeros((tok_rows, width), jnp.bfloat16)
    wide_zeros = jnp.zeros((micro_count, tok_rows, width), jnp.bfloat16)
    narrow_zeros = jnp.zeros((micro_count, tok_rows, rank_width), jnp.bfloat16)
    stores = (wide_zeros,)

    def forward_tick(moment, carried):
        received, holders = carried
        micro = moment - position
        active = (micro >= 0) & (micro < micro_count)
        slot = jnp.clip(micro, 0, micro_count - 1)
        fresh = lax.dynamic_index_in_dim(inputs, slot, 0, keepdims=False)
        entering = jnp.where(position == 0, fresh, received)

        def forward_run_section(holders):
            leaving, normed, before, activated = section_forward(
                entering, gain_row, full_in, full_out
            )
            contents = (entering,)
            return (leaving, write_slot(holders, contents, slot))

        def forward_skip_section(holders):
            return (blank, holders)

        leaving, holders = lax.cond(active, forward_run_section, forward_skip_section, holders)
        received = from_behind(leaving, "section", 1)
        return (received, holders)

    received, stores = lax.fori_loop(0, tick_total, forward_tick, (blank, stores))
    keep_rows = jnp.arange(tok_rows, dtype=jnp.int32)[None, :] < lengths[0][:, None]
    seeds = jnp.where(keep_rows[:, :, None], cotangent, jnp.zeros((), jnp.bfloat16))
    gain_start = jnp.zeros((width,), jnp.float32)
    buffers = (wide_zeros, narrow_zeros, wide_zeros, wide_zeros, narrow_zeros)

    def backward_tick(moment, carried):
        received, holders, gain_total = carried
        micro = moment - (section_count - 1 - position)
        active = (micro >= 0) & (micro < micro_count)
        slot = jnp.clip(micro, 0, micro_count - 1)
        seed_rows = lax.dynamic_index_in_dim(seeds, slot, 0, keepdims=False)
        entering = jnp.where(position == section_count - 1, seed_rows, received)

        def backward_run_section(operands):
            holders, gain_total = operands
            hidden_rows = lax.dynamic_index_in_dim(stores[0], slot, 0, keepdims=False)
            unused, normed, before, activated = section_forward(
                hidden_rows, gain_row, full_in, full_out
            )
            grad_hidden, grad_before, gain_terms = section_backward(
                hidden_rows, gain_row, full_in, full_out, before, entering
            )
            contents = (grad_hidden, grad_before, entering, normed, activated)
            return (grad_hidden, (write_slot(holders, contents, slot), gain_total + gain_terms))

        def backward_skip_section(operands):
            return (blank, operands)

        leaving, (holders, gain_total) = lax.cond(
            active, backward_run_section, backward_skip_section, (holders, gain_total)
        )
        received = from_behind(leaving, "section", -1)
        return (received, holders, gain_total)

    received, buffers, gain_total = lax.fori_loop(
        0, tick_total, backward_tick, (blank, buffers, gain_start)
    )
    normed_all = buffers[3]
    activated_all = buffers[4]
    flat_rows = micro_count * tok_rows
    normed_flat = normed_all.reshape(flat_rows, width)
    upstream_flat = buffers[2].reshape(flat_rows, width)
    before_flat = buffers[1].reshape(flat_rows, rank_width)
    activated_flat = activated_all.reshape(flat_rows, rank_width)
    left_term = lax.dot_general(
        normed_flat, before_flat, (((0,), (0,)), ((), ())), preferred_element_type=jnp.float32
    )
    right_term = lax.dot_general(
        upstream_flat, activated_flat, (((0,), (0,)), ((), ())), preferred_element_type=jnp.float32
    )
    summed = lax.psum_scatter(
        (jnp.concatenate((left_term, right_term), axis=1) * grad_scale).astype(jnp.bfloat16),
        "rep",
        scatter_dimension=0,
        tiled=True,
    ).astype(jnp.float32)
    grad_in_weight = summed[:, :rank_width].astype(jnp.bfloat16)[None]
    grad_out_weight = summed[:, rank_width:].astype(jnp.bfloat16)[None]
    grad_gain = lax.psum(gain_total * grad_scale, "rep")[None]
    grad_inputs = buffers[0][None]
    return (grad_in_weight, grad_out_weight, grad_gain, grad_inputs)


MESH = pl.DeviceIdType.MESH
contract_last = (((1,), (1,)), ((), ()))
contract_rows = (((0,), (0,)), ((), ()))
carrier = 128


def two_halves(column):
    high = column.astype(jnp.bfloat16).astype(jnp.float32)
    low = column - high
    lane = lax.broadcasted_iota(jnp.int32, (column.shape[0], carrier), 1)
    return jnp.where(lane == 0, high, jnp.where(lane == 1, low, 0.0)).astype(jnp.bfloat16)


def window_kernel(
    sections, replicas, grad_scale,
    x_ref, c_ref, wg_ref, wo_ref, raw_ref, gain_ref,
    gin_ref, gout_ref, gain_out_ref, rows_out_ref,
    hid, up, wgb, wob, fs_out, fs_pair, fs_mid, fs_in, bs_out, bs_pair, bs_mid, bs_in,
    act, gbi, before, inverse, m_out, n_out, m_tree, n_tree, m_in, n_in, land, gain_own,
    x_send, x_recv, c_send, c_recv, wg_send, wg_recv, wo_send, wo_recv,
    fp_send, fp_recv, bp_send, bp_recv, fs_send, fs_recv, bs_send, bs_recv,
    fg_send, fg_recv, fh_send, fh_recv, bg_send, bg_recv, bh_send, bh_recv,
    mt_send, mt_recv, m_send, m_recv, nt_send, nt_recv, n_send, n_recv,
    r_send, r_recv, q_send, q_recv, own_sem, g_send, g_recv,
):
    chunk, block = x_ref.shape[0], x_ref.shape[1] // replicas
    rank = wg_ref.shape[1]
    width = block * replicas
    sec, rep = lax.axis_index("section"), lax.axis_index("rep")

    stops = replicas // 2
    stop, core = rep // 2, lax.rem(rep, 2)
    partner = stop * 2 + 1 - core
    group = stops * chunk

    def spot(i):
        return pl.ds(pl.multiple_of(i * chunk, 16), chunk)

    def place(r):
        return spot(lax.rem(r, 2) * stops + r // 2)

    def half(c):
        return pl.ds(pl.multiple_of(c * group, 16), group)

    def lanes(r):
        return pl.ds(pl.multiple_of(r * block, 128), block)

    def to_rep(src, dst, send, recv, peer):
        return pltpu.make_async_remote_copy(
            src_ref=src, dst_ref=dst, send_sem=send, recv_sem=recv,
            device_id={"section": sec, "rep": peer}, device_id_type=MESH,
        )

    def to_sec(src, dst, send, recv, peer):
        return pltpu.make_async_remote_copy(
            src_ref=src, dst_ref=dst, send_sem=send, recv_sem=recv,
            device_id={"section": peer, "rep": rep}, device_id_type=MESH,
        )

    def each_rep(step):
        def go(i, carry):
            step(lax.rem(rep + i, replicas))
            return carry
        lax.fori_loop(1, replicas, go, 0)

    def each_stop(step):
        def go(i, carry):
            step(lax.rem(stop + i, stops))
            return carry
        lax.fori_loop(1, stops, go, 0)

    def each_sec(step):
        def go(i, carry):
            step(lax.rem(sec + i, sections))
            return carry
        lax.fori_loop(1, sections, go, 0)

    barrier = pltpu.get_barrier_semaphore()
    count = sections * replicas
    mine = sec * replicas + rep

    def greet(i, carry):
        other = lax.rem(mine + i, count)
        pl.semaphore_signal(
            barrier, inc=1,
            device_id={"section": other // replicas, "rep": lax.rem(other, replicas)},
            device_id_type=MESH,
        )
        return carry

    lax.fori_loop(1, count, greet, 0)
    pl.semaphore_wait(barrier, count - 1)

    def x_copy(peer, source):
        return to_rep(x_ref.at[:, lanes(peer)], hid.at[0, place(source)], x_send.at[peer], x_recv.at[source], peer)

    def c_copy(peer, source):
        return to_rep(
            c_ref.at[:, lanes(peer)], up.at[sections, place(source)], c_send.at[peer], c_recv.at[source], peer
        )

    def wg_copy(peer, source):
        return to_sec(wg_ref, wgb.at[source], wg_send.at[peer], wg_recv.at[source], peer)

    def wo_copy(peer, source):
        return to_sec(wo_ref, wob.at[source], wo_send.at[peer], wo_recv.at[source], peer)

    each_rep(lambda peer: x_copy(peer, rep).start())
    each_sec(lambda peer: wg_copy(peer, sec).start())
    each_sec(lambda peer: wo_copy(peer, sec).start())
    hid[0, place(rep)] = x_ref[:, lanes(rep)]
    up[sections, place(rep)] = c_ref[:, lanes(rep)]
    wgb[sec] = wg_ref[...]
    wob[sec] = wo_ref[...]
    each_rep(lambda peer: x_copy(peer, peer).wait_recv())
    each_rep(lambda peer: c_copy(peer, rep).start())

    class Sum:
        def __init__(self, out, pair, mid, landing, p_send, p_recv, z_send, z_recv):
            self.refs = out, pair, mid, landing
            self.sems = p_send, p_recv, z_send, z_recv

        def pair_copy(self, s):
            out, pair, _, _ = self.refs
            p_send, p_recv, _, _ = self.sems
            return to_rep(out.at[s, half(1 - core)], pair.at[s], p_send.at[s], p_recv.at[s], partner)

        def line_copy(self, s, peer, source):
            _, _, mid, landing = self.refs
            _, _, z_send, z_recv = self.sems
            return to_rep(
                mid.at[s, spot(peer)], landing.at[s, source],
                z_send.at[s, peer], z_recv.at[s, source], peer * 2 + core,
            )

        def start(self, s):
            self.pair_copy(s).start()

        def middle(self, s):
            out, pair, mid, _ = self.refs
            self.pair_copy(s).wait_recv()
            both = out[s, half(core)].astype(jnp.float32) + pair[s].astype(jnp.float32)
            mid[s] = both.astype(jnp.bfloat16)
            each_stop(lambda peer: self.line_copy(s, peer, stop).start())

        def finish(self, s):
            _, _, mid, landing = self.refs

            def go(i, total):
                source = lax.rem(stop + i, stops)
                self.line_copy(s, source, source).wait_recv()
                return total + landing[s, source].astype(jnp.float32)
            return lax.fori_loop(1, stops, go, mid[s, spot(stop)].astype(jnp.float32))

        def drain(self, s):
            self.pair_copy(s).wait_send()
            each_stop(lambda peer: self.line_copy(s, peer, stop).wait_send())

    class Spread:
        def __init__(self, ref, z_send, z_recv, p_send, p_recv):
            self.ref = ref
            self.sems = z_send, z_recv, p_send, p_recv

        def line_copy(self, s, peer, source):
            z_send, z_recv, _, _ = self.sems
            view = self.ref.at[s, place(source * 2 + core)]
            return to_rep(view, view, z_send.at[s, peer], z_recv.at[s, source], peer * 2 + core)

        def pair_copy(self, s, place_of, held):
            _, _, p_send, p_recv = self.sems
            view = self.ref.at[s, place(place_of * 2 + held)]
            return to_rep(view, view, p_send.at[s, place_of], p_recv.at[s, place_of], partner)

        def start(self, s):
            each_stop(lambda peer: self.line_copy(s, peer, stop).start())
            self.pair_copy(s, stop, core).start()

        def finish(self, s):
            def relay(source):
                self.line_copy(s, source, source).wait_recv()
                self.pair_copy(s, source, core).start()
            each_stop(relay)

            def arrive(i, carry):
                self.pair_copy(s, i, 1 - core).wait_recv()
                return carry
            lax.fori_loop(0, stops, arrive, 0)

        def drain(self, s):
            each_stop(lambda peer: self.line_copy(s, peer, stop).wait_send())

            def gone(i, carry):
                self.pair_copy(s, i, core).wait_send()
                return carry
            lax.fori_loop(0, stops, gone, 0)

    forward_sum = Sum(fs_out, fs_pair, fs_mid, fs_in, fp_send, fp_recv, fs_send, fs_recv)
    backward_sum = Sum(bs_out, bs_pair, bs_mid, bs_in, bp_send, bp_recv, bs_send, bs_recv)
    act_spread = Spread(act, fg_send, fg_recv, fh_send, fh_recv)
    gbi_spread = Spread(gbi, bg_send, bg_recv, bh_send, bh_recv)

    flip_x = sec // 2 * 2 + 1 - lax.rem(sec, 2)
    flip_y = (1 - sec // 2) * 2 + lax.rem(sec, 2)

    def relation(s):
        return lax.rem(sec // 2 + s // 2, 2) * 2 + lax.rem(sec + s, 2)

    class Tree:
        def __init__(self, out, tree, landing, t_send, t_recv, o_send, o_recv):
            self.refs = out, tree, landing
            self.sems = t_send, t_recv, o_send, o_recv

        def part(self, i):
            return pl.ds(i * (block // 2), block // 2)

        def corner_copy(self, s, i):
            out, tree, _ = self.refs
            t_send, t_recv, _, _ = self.sems
            return to_sec(
                out.at[s, self.part(i)], tree.at[s], t_send.at[s, i], t_recv.at[s], (flip_x, flip_y)[i]
            )

        def owner_copy(self, s, side, i):
            out, _, landing = self.refs
            _, _, o_send, o_recv = self.sems
            return to_sec(
                out.at[s, self.part(i)], landing.at[side, self.part(i)],
                o_send.at[s, i], o_recv.at[side, i], s,
            )

        def start(self, s):
            near = relation(s)

            @pl.when(near == 3)
            def _():
                self.corner_copy(s, 0).start()
                self.corner_copy(s, 1).start()

            for side in range(2):
                @pl.when(near == side + 1)
                def _():
                    self.owner_copy(s, side, side).start()

        def relay(self, s):
            near = relation(s)
            out, tree, _ = self.refs
            for side in range(2):
                @pl.when(near == side + 1)
                def _():
                    other = 1 - side
                    self.corner_copy(s, other).wait_recv()
                    out[s, self.part(other)] = (
                        out[s, self.part(other)].astype(jnp.float32) + tree[s].astype(jnp.float32)
                    ).astype(jnp.bfloat16)
                    self.owner_copy(s, side, other).start()

        def finish(self):
            out, _, landing = self.refs
            for side in range(2):
                for i in range(2):
                    self.owner_copy(sec, side, i).wait_recv()
            total = out[sec].astype(jnp.float32)
            for side in range(2):
                total = total + landing[side].astype(jnp.float32)
            return total * grad_scale

        def drain(self, s):
            near = relation(s)

            @pl.when(near == 3)
            def _():
                self.corner_copy(s, 0).wait_send()
                self.corner_copy(s, 1).wait_send()

            for side in range(2):
                @pl.when(near == side + 1)
                def _():
                    self.owner_copy(s, side, 0).wait_send()
                    self.owner_copy(s, side, 1).wait_send()

    m_way = Tree(m_out, m_tree, m_in, mt_send, mt_recv, m_send, m_recv)
    n_way = Tree(n_out, n_tree, n_in, nt_send, nt_recv, n_send, n_recv)

    def forward_send(s):
        @pl.when(s != sec)
        def _():
            wg_copy(s, s).wait_recv()

        hidden = hid[s]
        partial = jnp.dot(hidden, wgb[s], preferred_element_type=jnp.float32)
        fs_out[s, :, pl.ds(0, rank)] = partial.astype(jnp.bfloat16)
        widened = hidden.astype(jnp.float32)
        fs_out[s, :, pl.ds(rank, carrier)] = two_halves(jnp.sum(widened * widened, axis=1, keepdims=True))
        forward_sum.start(s)

    def forward_finish(s):
        total = forward_sum.finish(s)
        square = total[:, rank:rank + 1] + total[:, rank + 1:rank + 2]
        inv = lax.rsqrt(square / width + norm_epsilon)
        value = total[:, :rank] * inv
        before[s] = value
        inverse[s] = jnp.broadcast_to(inv, (chunk, carrier))
        act[s, place(rep)] = (value / (1.0 + jnp.exp(-value))).astype(jnp.bfloat16)
        act_spread.start(s)

    def wait_wo(s):
        @pl.when(s != sec)
        def _():
            wo_copy(s, s).wait_recv()

    def backward_send(s):
        bs_out[s] = jnp.dot(up[s + 1], wob[s], preferred_element_type=jnp.float32).astype(jnp.bfloat16)
        backward_sum.start(s)

    def backward_finish(s):
        grad_activated = backward_sum.finish(s)
        value = before[s]
        inv = inverse[s][:, :1]
        sig = 1.0 / (1.0 + jnp.exp(-value))
        grad_before = grad_activated * sig * (1.0 + value * (1.0 - sig))
        share = inv * inv * jnp.sum(grad_before * value, axis=1, keepdims=True) / width
        gbi[s, place(rep), pl.ds(0, rank)] = (grad_before * inv).astype(jnp.bfloat16)
        gbi[s, place(rep), pl.ds(rank, carrier)] = two_halves(share)
        gbi_spread.start(s)

    def upstream_step(s):
        gbi_spread.finish(s)
        grads = gbi[s]
        tail = grads[:, rank:].astype(jnp.float32)
        share = tail[:, 0:1] + tail[:, 1:2]
        spread = lax.dot_general(grads[:, :rank], wgb[s], contract_last, preferred_element_type=jnp.float32)
        up[s] = (
            up[s + 1].astype(jnp.float32) + spread - hid[s].astype(jnp.float32) * share
        ).astype(jnp.bfloat16)

    def line_rows(s, r, source):
        return to_rep(up.at[s, place(r)], land.at[s, source], r_send.at[s, r], r_recv.at[s, source], r)

    def held_rows(s, source, own):
        return up.at[s, place(rep)] if own else land.at[s, source]

    def plane_rows(s, source, own, from_s):
        return to_sec(
            held_rows(s, source, own), rows_out_ref.at[spot(from_s), lanes(source)],
            q_send.at[s, source], q_recv.at[from_s, source], s,
        )

    def kept_rows(source, own):
        return pltpu.make_async_copy(
            held_rows(sec, source, own), rows_out_ref.at[spot(sec), lanes(source)], own_sem.at[source]
        )

    def send_rows(s, first, end):
        def go(i, carry):
            r = lax.rem(rep + i, replicas)
            line_rows(s, r, rep).start()
            return carry
        lax.fori_loop(first, end, go, 0)

    def pass_rows(s):
        def move(source, own):
            @pl.when(s == sec)
            def _():
                kept_rows(source, own).start()

            @pl.when(s != sec)
            def _():
                plane_rows(s, source, own, sec).start()

        move(rep, True)

        def go(source):
            line_rows(s, source, source).wait_recv()
            move(source, False)
        each_rep(go)

    def m_step(s):
        m_out[s] = lax.dot_general(
            hid[s], gbi[s, :, pl.ds(0, rank)], contract_rows, preferred_element_type=jnp.float32
        ).astype(jnp.bfloat16)

        m_way.start(s)

    def n_step(s):
        n_out[s] = lax.dot_general(
            up[s + 1], act[s], contract_rows, preferred_element_type=jnp.float32
        ).astype(jnp.bfloat16)

        n_way.start(s)

    def forward(s, carry):
        forward_send(s)
        forward_sum.middle(s)
        forward_finish(s)
        wait_wo(s)
        act_spread.finish(s)
        mixed = lax.dot_general(act[s], wob[s], contract_last, preferred_element_type=jnp.float32)
        hid[s + 1] = (hid[s].astype(jnp.float32) + mixed).astype(jnp.bfloat16)
        return carry

    lax.fori_loop(0, sections - 1, forward, 0)
    last = sections - 1
    forward_send(last)
    wait_wo(last)
    each_rep(lambda peer: c_copy(peer, peer).wait_recv())
    backward_send(last)
    forward_sum.middle(last)
    backward_sum.middle(last)
    forward_finish(last)
    backward_finish(last)
    upstream_step(last)
    act_spread.finish(last)
    middle = replicas // 2

    def backward(i, carry):
        s = last - i
        backward_send(s)
        backward_sum.middle(s)
        send_rows(s + 1, 1, middle)

        @pl.when(i == 1)
        def _():
            n_step(last)

        m_step(s + 1)
        n_step(s)

        @pl.when(i == 2)
        def _():
            n_way.relay(last)

        @pl.when(i >= 2)
        def _():
            m_way.relay(s + 2)
            n_way.relay(s + 1)

        backward_finish(s)
        send_rows(s + 1, middle, replicas)

        @pl.when(i >= 2)
        def _():
            pass_rows(s + 2)

        upstream_step(s)
        return carry

    lax.fori_loop(1, sections, backward, 0)
    send_rows(0, 1, replicas)
    m_step(0)
    n_way.relay(0)
    m_way.relay(1)
    m_way.relay(0)
    pass_rows(1)
    pass_rows(0)

    gout_ref[...] = n_way.finish().astype(jnp.bfloat16)
    product = m_way.finish()
    gin_ref[...] = (product * gain_ref[...]).astype(jnp.bfloat16)
    terms = product * raw_ref[...].astype(jnp.float32)
    high = terms.astype(jnp.bfloat16)
    low = (terms - high.astype(jnp.float32)).astype(jnp.bfloat16)
    ones = jnp.ones((8, rank), jnp.bfloat16)
    gain_own[...] = lax.dot_general(
        ones, high, contract_last, preferred_element_type=jnp.float32
    ) + lax.dot_general(ones, low, contract_last, preferred_element_type=jnp.float32)

    def g_copy(peer, source):
        return to_rep(
            gain_own, gain_out_ref.at[:, lanes(source)], g_send.at[peer], g_recv.at[source], peer
        )

    each_rep(lambda peer: g_copy(peer, rep).start())
    gain_out_ref[:, lanes(rep)] = gain_own[...]

    def each_section(step):
        def go(s, carry):
            step(s)
            return carry
        lax.fori_loop(0, sections, go, 0)

    def sent(s):
        forward_sum.drain(s)
        backward_sum.drain(s)
        act_spread.drain(s)
        gbi_spread.drain(s)
        m_way.drain(s)
        n_way.drain(s)
        each_rep(lambda peer: line_rows(s, peer, rep).wait_send())

        @pl.when(s != sec)
        def _():
            wg_copy(s, sec).wait_send()
            wo_copy(s, sec).wait_send()
            plane_rows(s, rep, True, sec).wait_send()
            plane_rows(sec, rep, True, s).wait_recv()
            each_rep(lambda source: plane_rows(s, source, False, sec).wait_send())
            each_rep(lambda source: plane_rows(sec, source, False, s).wait_recv())

    each_section(sent)
    kept_rows(rep, True).wait()
    each_rep(lambda source: kept_rows(source, False).wait())
    each_rep(lambda peer: x_copy(peer, rep).wait_send())
    each_rep(lambda peer: c_copy(peer, rep).wait_send())
    each_rep(lambda peer: g_copy(peer, rep).wait_send())
    each_rep(lambda peer: g_copy(peer, peer).wait_recv())


def window_body(inputs, cotangent, in_weight, out_weight, norm_gain, lengths):
    sections, replicas = lax.axis_size("section"), lax.axis_size("rep")
    sec, rep = lax.axis_index("section"), lax.axis_index("rep")
    micro_count, tok_rows, width = inputs.shape
    block, rank = in_weight.shape[1:]
    own_rows = micro_count * tok_rows
    chunk = own_rows // sections
    rows = chunk * replicas
    grad_scale = 1.0 / math.sqrt(own_rows * replicas)
    keep = jnp.arange(tok_rows, dtype=jnp.int32)[None, :] < lengths[0][:, None]

    def part(array):
        return lax.dynamic_slice_in_dim(array.reshape(own_rows, width), sec * chunk, chunk, 0)

    kept = lax.dynamic_slice_in_dim(keep.reshape(own_rows), sec * chunk, chunk, 0)
    x_parts = part(inputs)
    c_parts = jnp.where(kept[:, None], part(cotangent), jnp.zeros((), jnp.bfloat16))
    gain = lax.dynamic_slice_in_dim(norm_gain[0], rep * block, block, 0)[:, None]
    scaled = (in_weight[0].astype(jnp.float32) * gain).astype(jnp.bfloat16)
    bf, f32 = jnp.bfloat16, jnp.float32
    dma = pltpu.SemaphoreType.DMA
    vmem = pl.BlockSpec(memory_space=pltpu.VMEM)
    wide = rank + carrier
    stops = replicas // 2
    grad_in, grad_out, grad_gain, grad_rows = pl.pallas_call(
        functools.partial(window_kernel, sections, replicas, grad_scale),
        out_shape=(
            jax.ShapeDtypeStruct((block, rank), bf),
            jax.ShapeDtypeStruct((block, rank), bf),
            jax.ShapeDtypeStruct((8, width), f32),
            jax.ShapeDtypeStruct((own_rows, width), bf),
        ),
        in_specs=[vmem] * 6,
        out_specs=(vmem, vmem, vmem, pl.BlockSpec(memory_space=pl.ANY)),
        scratch_shapes=[
            pltpu.VMEM((sections, rows, block), bf),
            pltpu.VMEM((sections + 1, rows, block), bf),
            pltpu.VMEM((sections, block, rank), bf),
            pltpu.VMEM((sections, block, rank), bf),
            pltpu.VMEM((sections, rows, wide), bf),
            pltpu.VMEM((sections, rows // 2, wide), bf),
            pltpu.VMEM((sections, rows // 2, wide), bf),
            pltpu.VMEM((sections, stops, chunk, wide), bf),
            pltpu.VMEM((sections, rows, rank), bf),
            pltpu.VMEM((sections, rows // 2, rank), bf),
            pltpu.VMEM((sections, rows // 2, rank), bf),
            pltpu.VMEM((sections, stops, chunk, rank), bf),
            pltpu.VMEM((sections, rows, rank), bf),
            pltpu.VMEM((sections, rows, wide), bf),
            pltpu.VMEM((sections, chunk, rank), f32),
            pltpu.VMEM((sections, chunk, carrier), f32),
            *[pltpu.VMEM((sections, block, rank), bf)] * 2,
            *[pltpu.VMEM((sections, block // 2, rank), bf)] * 2,
            *[pltpu.VMEM((2, block, rank), bf)] * 2,
            pltpu.VMEM((sections, replicas, chunk, block), bf),
            pltpu.VMEM((8, block), f32),
            *[dma((replicas,))] * 4,
            *[dma((sections,))] * 4,
            *[dma((sections,))] * 4,
            *[dma((sections, stops))] * 12,
            *[dma((sections, 2)), dma((sections,)), dma((sections, 2)), dma((2, 2))] * 2,
            *[dma((sections, replicas))] * 4,
            *[dma((replicas,))] * 3,
        ],
        compiler_params=pltpu.CompilerParams(
            collective_id=0, has_side_effects=True, vmem_limit_bytes=60 * 1024 * 1024
        ),
        name="adapter_window",
    )(x_parts, c_parts, scaled, out_weight[0], in_weight[0], gain)
    return (
        grad_in[None],
        grad_out[None],
        grad_gain[:1],
        grad_rows.reshape(1, micro_count, tok_rows, width),
    )


def body(inputs, cotangent, in_weight, out_weight, norm_gain, lengths):
    sections = lax.axis_size("section")
    block, rank = in_weight.shape[1:]
    own_rows = inputs.shape[0] * inputs.shape[1]
    aligned = own_rows % (16 * sections) == 0 and block % 128 == 0 and rank % 128 == 0
    square = sections == 4 and lax.axis_size("rep") % 2 == 0
    chosen = window_body if aligned and square else staged_body
    return chosen(inputs, cotangent, in_weight, out_weight, norm_gain, lengths)


def solution(mesh):
    in_specs = (
        P(None, "rep", None),
        P(None, "rep", None),
        P("section", "rep", None),
        P("section", "rep", None),
        P("section", None),
        P("rep", None),
    )
    out_specs = (
        P("section", "rep", None),
        P("section", "rep", None),
        P("section", None),
        P("section", None, "rep", None),
    )
    return jax.shard_map(body, mesh=mesh, in_specs=in_specs, out_specs=out_specs, check_vma=False)
```

```python
import functools
import math

import jax
import jax.numpy as jnp
from jax import lax
from jax.experimental import pallas as pl
from jax.experimental.pallas import tpu as pltpu
from jax.sharding import PartitionSpec as P

norm_epsilon = 1e-05


def from_behind(block, axis, distance):
    devices = range(lax.axis_size(axis))
    route = [(i - distance, i) for i in devices if i - distance in devices]
    return lax.ppermute(block, axis, route)


def section_forward(hidden, norm_gain, in_weight, out_weight):
    widened = hidden.astype(jnp.float32)
    inverse = lax.rsqrt(jnp.mean(widened * widened, axis=-1, keepdims=True) + norm_epsilon)
    normed = (widened * inverse * norm_gain).astype(jnp.bfloat16)
    before = jnp.dot(normed, in_weight, preferred_element_type=jnp.float32)
    activated = jax.nn.silu(before).astype(jnp.bfloat16)
    mixed = lax.dot_general(
        activated, out_weight, (((1,), (1,)), ((), ())), preferred_element_type=jnp.float32
    )
    return ((widened + mixed).astype(jnp.bfloat16), normed, before, activated)


def section_backward(hidden, norm_gain, in_weight, out_weight, before, upstream):
    widened = hidden.astype(jnp.float32)
    inverse = lax.rsqrt(jnp.mean(widened * widened, axis=-1, keepdims=True) + norm_epsilon)
    grad_activated = jnp.dot(upstream, out_weight, preferred_element_type=jnp.float32)
    sigmoid_value = jax.nn.sigmoid(before)
    grad_before = (grad_activated * sigmoid_value * (1.0 + before * (1.0 - sigmoid_value))).astype(
        jnp.bfloat16
    )
    grad_normed = lax.dot_general(
        grad_before, in_weight, (((1,), (1,)), ((), ())), preferred_element_type=jnp.float32
    )
    grad_scaled = grad_normed * norm_gain
    projection = jnp.mean(grad_scaled * widened, axis=-1, keepdims=True)
    grad_hidden = (
        upstream.astype(jnp.float32)
        + inverse * grad_scaled
        - widened * (inverse * inverse * inverse) * projection
    )
    gain_terms = jnp.sum(grad_normed * widened * inverse, axis=0)
    return (grad_hidden.astype(jnp.bfloat16), grad_before, gain_terms)


def write_slot(holders, contents, slot):
    return tuple(
        (
            lax.dynamic_update_index_in_dim(holder, content, slot, 0)
            for holder, content in zip(holders, contents)
        )
    )


def staged_body(inputs, cotangent, in_weight, out_weight, norm_gain, lengths):
    section_count = lax.axis_size("section")
    replicas = lax.axis_size("rep")
    position = lax.axis_index("section")
    micro_count, tok_rows, width = inputs.shape
    grad_scale = 1.0 / math.sqrt(micro_count * tok_rows * replicas)
    gain_row = norm_gain[0]
    full_in, full_out = (
        lax.all_gather(in_weight[0], "rep", axis=0, tiled=True),
        lax.all_gather(out_weight[0], "rep", axis=0, tiled=True),
    )
    rank_width = full_in.shape[1]
    tick_total = micro_count + section_count - 1
    blank = jnp.zeros((tok_rows, width), jnp.bfloat16)
    wide_zeros = jnp.zeros((micro_count, tok_rows, width), jnp.bfloat16)
    narrow_zeros = jnp.zeros((micro_count, tok_rows, rank_width), jnp.bfloat16)
    stores = (wide_zeros,)

    def forward_tick(moment, carried):
        received, holders = carried
        micro = moment - position
        active = (micro >= 0) & (micro < micro_count)
        slot = jnp.clip(micro, 0, micro_count - 1)
        fresh = lax.dynamic_index_in_dim(inputs, slot, 0, keepdims=False)
        entering = jnp.where(position == 0, fresh, received)

        def forward_run_section(holders):
            leaving, normed, before, activated = section_forward(
                entering, gain_row, full_in, full_out
            )
            contents = (entering,)
            return (leaving, write_slot(holders, contents, slot))

        def forward_skip_section(holders):
            return (blank, holders)

        leaving, holders = lax.cond(active, forward_run_section, forward_skip_section, holders)
        received = from_behind(leaving, "section", 1)
        return (received, holders)

    received, stores = lax.fori_loop(0, tick_total, forward_tick, (blank, stores))
    keep_rows = jnp.arange(tok_rows, dtype=jnp.int32)[None, :] < lengths[0][:, None]
    seeds = jnp.where(keep_rows[:, :, None], cotangent, jnp.zeros((), jnp.bfloat16))
    gain_start = jnp.zeros((width,), jnp.float32)
    buffers = (wide_zeros, narrow_zeros, wide_zeros, wide_zeros, narrow_zeros)

    def backward_tick(moment, carried):
        received, holders, gain_total = carried
        micro = moment - (section_count - 1 - position)
        active = (micro >= 0) & (micro < micro_count)
        slot = jnp.clip(micro, 0, micro_count - 1)
        seed_rows = lax.dynamic_index_in_dim(seeds, slot, 0, keepdims=False)
        entering = jnp.where(position == section_count - 1, seed_rows, received)

        def backward_run_section(operands):
            holders, gain_total = operands
            hidden_rows = lax.dynamic_index_in_dim(stores[0], slot, 0, keepdims=False)
            unused, normed, before, activated = section_forward(
                hidden_rows, gain_row, full_in, full_out
            )
            grad_hidden, grad_before, gain_terms = section_backward(
                hidden_rows, gain_row, full_in, full_out, before, entering
            )
            contents = (grad_hidden, grad_before, entering, normed, activated)
            return (grad_hidden, (write_slot(holders, contents, slot), gain_total + gain_terms))

        def backward_skip_section(operands):
            return (blank, operands)

        leaving, (holders, gain_total) = lax.cond(
            active, backward_run_section, backward_skip_section, (holders, gain_total)
        )
        received = from_behind(leaving, "section", -1)
        return (received, holders, gain_total)

    received, buffers, gain_total = lax.fori_loop(
        0, tick_total, backward_tick, (blank, buffers, gain_start)
    )
    normed_all = buffers[3]
    activated_all = buffers[4]
    flat_rows = micro_count * tok_rows
    normed_flat = normed_all.reshape(flat_rows, width)
    upstream_flat = buffers[2].reshape(flat_rows, width)
    before_flat = buffers[1].reshape(flat_rows, rank_width)
    activated_flat = activated_all.reshape(flat_rows, rank_width)
    left_term = lax.dot_general(
        normed_flat, before_flat, (((0,), (0,)), ((), ())), preferred_element_type=jnp.float32
    )
    right_term = lax.dot_general(
        upstream_flat, activated_flat, (((0,), (0,)), ((), ())), preferred_element_type=jnp.float32
    )
    summed = lax.psum_scatter(
        (jnp.concatenate((left_term, right_term), axis=1) * grad_scale).astype(jnp.bfloat16),
        "rep",
        scatter_dimension=0,
        tiled=True,
    ).astype(jnp.float32)
    grad_in_weight = summed[:, :rank_width].astype(jnp.bfloat16)[None]
    grad_out_weight = summed[:, rank_width:].astype(jnp.bfloat16)[None]
    grad_gain = lax.psum(gain_total * grad_scale, "rep")[None]
    grad_inputs = buffers[0][None]
    return (grad_in_weight, grad_out_weight, grad_gain, grad_inputs)


MESH = pl.DeviceIdType.MESH
contract_last = (((1,), (1,)), ((), ()))
contract_rows = (((0,), (0,)), ((), ()))
carrier = 128


def two_halves(column):
    high = column.astype(jnp.bfloat16).astype(jnp.float32)
    low = column - high
    lane = lax.broadcasted_iota(jnp.int32, (column.shape[0], carrier), 1)
    return jnp.where(lane == 0, high, jnp.where(lane == 1, low, 0.0)).astype(jnp.bfloat16)


def window_kernel(
    sections, replicas, grad_scale,
    x_ref, c_ref, wg_ref, wo_ref, raw_ref, gain_ref,
    gin_ref, gout_ref, gain_out_ref, rows_out_ref,
    hid, up, wgb, wob, fs_out, fs_pair, fs_mid, fs_in, bs_out, bs_pair, bs_mid, bs_in,
    act, gbi, before, inverse, m_out, n_out, m_tree, n_tree, m_in, n_in, land, far, gain_own,
    x_send, x_recv, c_send, c_recv, wg_send, wg_recv, wo_send, wo_recv,
    fp_send, fp_recv, bp_send, bp_recv, fs_send, fs_recv, bs_send, bs_recv,
    fg_send, fg_recv, fh_send, fh_recv, bg_send, bg_recv, bh_send, bh_recv,
    mt_send, mt_recv, m_send, m_recv, nt_send, nt_recv, n_send, n_recv,
    r_send, r_recv, q_send, q_recv, v_send, v_recv, w_send, own_sem, g_send, g_recv,
):
    chunk, block = x_ref.shape[0], x_ref.shape[1] // replicas
    rank = wg_ref.shape[1]
    width = block * replicas
    sec, rep = lax.axis_index("section"), lax.axis_index("rep")

    stops = replicas // 2
    stop, core = rep // 2, lax.rem(rep, 2)
    partner = stop * 2 + 1 - core
    group = stops * chunk
    middle = replicas // 2

    def spot(i):
        return pl.ds(pl.multiple_of(i * chunk, 16), chunk)

    def place(r):
        return spot(lax.rem(r, 2) * stops + r // 2)

    def half(c):
        return pl.ds(pl.multiple_of(c * group, 16), group)

    def lanes(r):
        return pl.ds(pl.multiple_of(r * block, 128), block)

    def to_rep(src, dst, send, recv, peer):
        return pltpu.make_async_remote_copy(
            src_ref=src, dst_ref=dst, send_sem=send, recv_sem=recv,
            device_id={"section": sec, "rep": peer}, device_id_type=MESH,
        )

    def to_sec(src, dst, send, recv, peer):
        return pltpu.make_async_remote_copy(
            src_ref=src, dst_ref=dst, send_sem=send, recv_sem=recv,
            device_id={"section": peer, "rep": rep}, device_id_type=MESH,
        )

    def each_rep(step):
        def go(i, carry):
            step(lax.rem(rep + i, replicas))
            return carry
        lax.fori_loop(1, replicas, go, 0)

    def each_stop(step):
        def go(i, carry):
            step(lax.rem(stop + i, stops))
            return carry
        lax.fori_loop(1, stops, go, 0)

    def each_sec(step):
        def go(i, carry):
            step(lax.rem(sec + i, sections))
            return carry
        lax.fori_loop(1, sections, go, 0)

    barrier = pltpu.get_barrier_semaphore()
    count = sections * replicas
    mine = sec * replicas + rep

    def greet(i, carry):
        other = lax.rem(mine + i, count)
        pl.semaphore_signal(
            barrier, inc=1,
            device_id={"section": other // replicas, "rep": lax.rem(other, replicas)},
            device_id_type=MESH,
        )
        return carry

    lax.fori_loop(1, count, greet, 0)
    pl.semaphore_wait(barrier, count - 1)

    def x_copy(peer, source):
        return to_rep(x_ref.at[:, lanes(peer)], hid.at[0, place(source)], x_send.at[peer], x_recv.at[source], peer)

    def c_copy(peer, source):
        return to_rep(
            c_ref.at[:, lanes(peer)], up.at[sections, place(source)], c_send.at[peer], c_recv.at[source], peer
        )

    def wg_copy(peer, source):
        return to_sec(wg_ref, wgb.at[source], wg_send.at[peer], wg_recv.at[source], peer)

    def wo_copy(peer, source):
        return to_sec(wo_ref, wob.at[source], wo_send.at[peer], wo_recv.at[source], peer)

    each_rep(lambda peer: x_copy(peer, rep).start())
    each_sec(lambda peer: wg_copy(peer, sec).start())
    each_sec(lambda peer: wo_copy(peer, sec).start())
    hid[0, place(rep)] = x_ref[:, lanes(rep)]
    up[sections, place(rep)] = c_ref[:, lanes(rep)]
    wgb[sec] = wg_ref[...]
    wob[sec] = wo_ref[...]
    each_rep(lambda peer: x_copy(peer, peer).wait_recv())
    each_rep(lambda peer: c_copy(peer, rep).start())

    class Sum:
        def __init__(self, out, pair, mid, landing, p_send, p_recv, z_send, z_recv):
            self.refs = out, pair, mid, landing
            self.sems = p_send, p_recv, z_send, z_recv

        def pair_copy(self, s):
            out, pair, _, _ = self.refs
            p_send, p_recv, _, _ = self.sems
            return to_rep(out.at[s, half(1 - core)], pair.at[s], p_send.at[s], p_recv.at[s], partner)

        def line_copy(self, s, peer, source):
            _, _, mid, landing = self.refs
            _, _, z_send, z_recv = self.sems
            return to_rep(
                mid.at[s, spot(peer)], landing.at[s, source],
                z_send.at[s, peer], z_recv.at[s, source], peer * 2 + core,
            )

        def start(self, s):
            self.pair_copy(s).start()

        def middle(self, s):
            out, pair, mid, _ = self.refs
            self.pair_copy(s).wait_recv()
            both = out[s, half(core)].astype(jnp.float32) + pair[s].astype(jnp.float32)
            mid[s] = both.astype(jnp.bfloat16)
            each_stop(lambda peer: self.line_copy(s, peer, stop).start())

        def finish(self, s):
            _, _, mid, landing = self.refs

            def go(i, total):
                source = lax.rem(stop + i, stops)
                self.line_copy(s, source, source).wait_recv()
                return total + landing[s, source].astype(jnp.float32)
            return lax.fori_loop(1, stops, go, mid[s, spot(stop)].astype(jnp.float32))

        def drain(self, s):
            self.pair_copy(s).wait_send()
            each_stop(lambda peer: self.line_copy(s, peer, stop).wait_send())

    class Spread:
        def __init__(self, ref, z_send, z_recv, p_send, p_recv):
            self.ref = ref
            self.sems = z_send, z_recv, p_send, p_recv

        def line_copy(self, s, peer, source):
            z_send, z_recv, _, _ = self.sems
            view = self.ref.at[s, place(source * 2 + core)]
            return to_rep(view, view, z_send.at[s, peer], z_recv.at[s, source], peer * 2 + core)

        def pair_copy(self, s, place_of, held):
            _, _, p_send, p_recv = self.sems
            view = self.ref.at[s, place(place_of * 2 + held)]
            return to_rep(view, view, p_send.at[s, place_of], p_recv.at[s, place_of], partner)

        def start(self, s):
            each_stop(lambda peer: self.line_copy(s, peer, stop).start())
            self.pair_copy(s, stop, core).start()

        def finish(self, s):
            def relay(source):
                self.line_copy(s, source, source).wait_recv()
                self.pair_copy(s, source, core).start()
            each_stop(relay)

            def arrive(i, carry):
                self.pair_copy(s, i, 1 - core).wait_recv()
                return carry
            lax.fori_loop(0, stops, arrive, 0)

        def drain(self, s):
            each_stop(lambda peer: self.line_copy(s, peer, stop).wait_send())

            def gone(i, carry):
                self.pair_copy(s, i, core).wait_send()
                return carry
            lax.fori_loop(0, stops, gone, 0)

    forward_sum = Sum(fs_out, fs_pair, fs_mid, fs_in, fp_send, fp_recv, fs_send, fs_recv)
    backward_sum = Sum(bs_out, bs_pair, bs_mid, bs_in, bp_send, bp_recv, bs_send, bs_recv)
    act_spread = Spread(act, fg_send, fg_recv, fh_send, fh_recv)
    gbi_spread = Spread(gbi, bg_send, bg_recv, bh_send, bh_recv)

    flip_x = sec // 2 * 2 + 1 - lax.rem(sec, 2)
    flip_y = (1 - sec // 2) * 2 + lax.rem(sec, 2)

    def relation(s):
        return lax.rem(sec // 2 + s // 2, 2) * 2 + lax.rem(sec + s, 2)

    class Tree:
        def __init__(self, out, tree, landing, t_send, t_recv, o_send, o_recv):
            self.refs = out, tree, landing
            self.sems = t_send, t_recv, o_send, o_recv

        def part(self, i):
            return pl.ds(i * (block // 2), block // 2)

        def corner_copy(self, s, i):
            out, tree, _ = self.refs
            t_send, t_recv, _, _ = self.sems
            return to_sec(
                out.at[s, self.part(i)], tree.at[s], t_send.at[s, i], t_recv.at[s], (flip_x, flip_y)[i]
            )

        def owner_copy(self, s, side, i):
            out, _, landing = self.refs
            _, _, o_send, o_recv = self.sems
            return to_sec(
                out.at[s, self.part(i)], landing.at[side, self.part(i)],
                o_send.at[s, i], o_recv.at[side, i], s,
            )

        def start(self, s):
            near = relation(s)

            @pl.when(near == 3)
            def _():
                self.corner_copy(s, 0).start()
                self.corner_copy(s, 1).start()

            for side in range(2):
                @pl.when(near == side + 1)
                def _():
                    self.owner_copy(s, side, side).start()

        def relay(self, s):
            near = relation(s)
            out, tree, _ = self.refs
            for side in range(2):
                @pl.when(near == side + 1)
                def _():
                    other = 1 - side
                    self.corner_copy(s, other).wait_recv()
                    out[s, self.part(other)] = (
                        out[s, self.part(other)].astype(jnp.float32) + tree[s].astype(jnp.float32)
                    ).astype(jnp.bfloat16)
                    self.owner_copy(s, side, other).start()

        def finish(self):
            out, _, landing = self.refs
            for side in range(2):
                for i in range(2):
                    self.owner_copy(sec, side, i).wait_recv()
            total = out[sec].astype(jnp.float32)
            for side in range(2):
                total = total + landing[side].astype(jnp.float32)
            return total * grad_scale

        def drain(self, s):
            near = relation(s)

            @pl.when(near == 3)
            def _():
                self.corner_copy(s, 0).wait_send()
                self.corner_copy(s, 1).wait_send()

            for side in range(2):
                @pl.when(near == side + 1)
                def _():
                    self.owner_copy(s, side, 0).wait_send()
                    self.owner_copy(s, side, 1).wait_send()

    m_way = Tree(m_out, m_tree, m_in, mt_send, mt_recv, m_send, m_recv)
    n_way = Tree(n_out, n_tree, n_in, nt_send, nt_recv, n_send, n_recv)

    def forward_send(s):
        @pl.when(s != sec)
        def _():
            wg_copy(s, s).wait_recv()

        hidden = hid[s]
        partial = jnp.dot(hidden, wgb[s], preferred_element_type=jnp.float32)
        fs_out[s, :, pl.ds(0, rank)] = partial.astype(jnp.bfloat16)
        widened = hidden.astype(jnp.float32)
        fs_out[s, :, pl.ds(rank, carrier)] = two_halves(jnp.sum(widened * widened, axis=1, keepdims=True))
        forward_sum.start(s)

    def forward_finish(s):
        total = forward_sum.finish(s)
        square = total[:, rank:rank + 1] + total[:, rank + 1:rank + 2]
        inv = lax.rsqrt(square / width + norm_epsilon)
        value = total[:, :rank] * inv
        before[s] = value
        inverse[s] = jnp.broadcast_to(inv, (chunk, carrier))
        act[s, place(rep)] = (value / (1.0 + jnp.exp(-value))).astype(jnp.bfloat16)
        act_spread.start(s)

    def wait_wo(s):
        @pl.when(s != sec)
        def _():
            wo_copy(s, s).wait_recv()

    def backward_send(s):
        bs_out[s] = jnp.dot(up[s + 1], wob[s], preferred_element_type=jnp.float32).astype(jnp.bfloat16)
        backward_sum.start(s)

    def backward_finish(s):
        grad_activated = backward_sum.finish(s)
        value = before[s]
        inv = inverse[s][:, :1]
        sig = 1.0 / (1.0 + jnp.exp(-value))
        grad_before = grad_activated * sig * (1.0 + value * (1.0 - sig))
        share = inv * inv * jnp.sum(grad_before * value, axis=1, keepdims=True) / width
        gbi[s, place(rep), pl.ds(0, rank)] = (grad_before * inv).astype(jnp.bfloat16)
        gbi[s, place(rep), pl.ds(rank, carrier)] = two_halves(share)
        gbi_spread.start(s)

    def upstream_step(s):
        gbi_spread.finish(s)
        grads = gbi[s]
        tail = grads[:, rank:].astype(jnp.float32)
        share = tail[:, 0:1] + tail[:, 1:2]
        spread = lax.dot_general(grads[:, :rank], wgb[s], contract_last, preferred_element_type=jnp.float32)
        up[s] = (
            up[s + 1].astype(jnp.float32) + spread - hid[s].astype(jnp.float32) * share
        ).astype(jnp.bfloat16)

    def line_rows(s, r, source):
        return to_rep(up.at[s, place(r)], land.at[s, source], r_send.at[s, r], r_recv.at[s, source], r)

    def held_rows(s, source, own):
        return up.at[s, place(rep)] if own else land.at[s, source]

    def plane_rows(s, source, own, from_s):
        return to_sec(
            held_rows(s, source, own), rows_out_ref.at[spot(from_s), lanes(source)],
            q_send.at[s, source], q_recv.at[from_s, source], s,
        )

    def corner_rows(s, source, own):
        side = source // middle
        slot = lax.rem(source, middle)
        return to_sec(
            held_rows(s, source, own), far.at[s, slot], v_send.at[s, source], v_recv.at[s, slot],
            flip_y + side * (flip_x - flip_y),
        )

    def onward_rows(s, side, slot):
        source, origin = side * middle + slot, (flip_y, flip_x)[side]
        return to_sec(
            far.at[s, slot], rows_out_ref.at[spot(origin), lanes(source)],
            w_send.at[s, slot], q_recv.at[origin, source], s,
        )

    def relay_rows(s):
        near = relation(s)
        for side in range(2):
            @pl.when(near == side + 1)
            def _():
                def go(slot, carry):
                    arrived = to_sec(far.at[s, slot], far.at[s, slot], v_send.at[s, 0], v_recv.at[s, slot], s)
                    arrived.wait_recv()
                    onward_rows(s, side, slot).start()
                    return carry
                lax.fori_loop(0, middle, go, 0)

    def kept_rows(source, own):
        return pltpu.make_async_copy(
            held_rows(sec, source, own), rows_out_ref.at[spot(sec), lanes(source)], own_sem.at[source]
        )

    def send_rows(s, first, end):
        def go(i, carry):
            r = lax.rem(rep + i, replicas)
            line_rows(s, r, rep).start()
            return carry
        lax.fori_loop(first, end, go, 0)

    def pass_rows(s):
        def move(source, own):
            @pl.when(s == sec)
            def _():
                kept_rows(source, own).start()

            near = relation(s)

            @pl.when((near == 1) | (near == 2))
            def _():
                plane_rows(s, source, own, sec).start()

            @pl.when(near == 3)
            def _():
                corner_rows(s, source, own).start()

        move(rep, True)

        def go(source):
            line_rows(s, source, source).wait_recv()
            move(source, False)
        each_rep(go)

    def m_step(s):
        m_out[s] = lax.dot_general(
            hid[s], gbi[s, :, pl.ds(0, rank)], contract_rows, preferred_element_type=jnp.float32
        ).astype(jnp.bfloat16)

        m_way.start(s)

    def n_step(s):
        n_out[s] = lax.dot_general(
            up[s + 1], act[s], contract_rows, preferred_element_type=jnp.float32
        ).astype(jnp.bfloat16)

        n_way.start(s)

    def forward(s, carry):
        forward_send(s)
        forward_sum.middle(s)
        forward_finish(s)
        wait_wo(s)
        act_spread.finish(s)
        mixed = lax.dot_general(act[s], wob[s], contract_last, preferred_element_type=jnp.float32)
        hid[s + 1] = (hid[s].astype(jnp.float32) + mixed).astype(jnp.bfloat16)
        return carry

    lax.fori_loop(0, sections - 1, forward, 0)
    last = sections - 1
    forward_send(last)
    wait_wo(last)
    each_rep(lambda peer: c_copy(peer, peer).wait_recv())
    backward_send(last)
    forward_sum.middle(last)
    backward_sum.middle(last)
    forward_finish(last)
    backward_finish(last)
    upstream_step(last)
    act_spread.finish(last)

    def backward(i, carry):
        s = last - i
        backward_send(s)
        backward_sum.middle(s)
        send_rows(s + 1, 1, middle)

        @pl.when(i == 1)
        def _():
            n_step(last)

        m_step(s + 1)
        n_step(s)

        @pl.when(i == 2)
        def _():
            n_way.relay(last)

        @pl.when(i >= 2)
        def _():
            m_way.relay(s + 2)
            n_way.relay(s + 1)

        backward_finish(s)
        send_rows(s + 1, middle, replicas)

        @pl.when(i >= 2)
        def _():
            pass_rows(s + 2)

        @pl.when(i >= 3)
        def _():
            relay_rows(s + 3)

        upstream_step(s)
        return carry

    lax.fori_loop(1, sections, backward, 0)
    send_rows(0, 1, replicas)
    m_step(0)
    n_way.relay(0)
    m_way.relay(1)
    m_way.relay(0)
    pass_rows(1)
    relay_rows(2)
    pass_rows(0)
    relay_rows(1)
    relay_rows(0)

    gout_ref[...] = n_way.finish().astype(jnp.bfloat16)
    product = m_way.finish()
    gin_ref[...] = (product * gain_ref[...]).astype(jnp.bfloat16)
    terms = product * raw_ref[...].astype(jnp.float32)
    high = terms.astype(jnp.bfloat16)
    low = (terms - high.astype(jnp.float32)).astype(jnp.bfloat16)
    ones = jnp.ones((8, rank), jnp.bfloat16)
    gain_own[...] = lax.dot_general(
        ones, high, contract_last, preferred_element_type=jnp.float32
    ) + lax.dot_general(ones, low, contract_last, preferred_element_type=jnp.float32)

    def g_copy(peer, source):
        return to_rep(
            gain_own, gain_out_ref.at[:, lanes(source)], g_send.at[peer], g_recv.at[source], peer
        )

    each_rep(lambda peer: g_copy(peer, rep).start())
    gain_out_ref[:, lanes(rep)] = gain_own[...]

    def each_section(step):
        def go(s, carry):
            step(s)
            return carry
        lax.fori_loop(0, sections, go, 0)

    def sent(s):
        forward_sum.drain(s)
        backward_sum.drain(s)
        act_spread.drain(s)
        gbi_spread.drain(s)
        m_way.drain(s)
        n_way.drain(s)
        each_rep(lambda peer: line_rows(s, peer, rep).wait_send())

        @pl.when(s != sec)
        def _():
            wg_copy(s, sec).wait_send()
            wo_copy(s, sec).wait_send()
            plane_rows(sec, rep, True, s).wait_recv()
            each_rep(lambda source: plane_rows(sec, source, False, s).wait_recv())

        near = relation(s)

        @pl.when(near == 3)
        def _():
            corner_rows(s, rep, True).wait_send()
            each_rep(lambda source: corner_rows(s, source, False).wait_send())

        for side in range(2):
            @pl.when(near == side + 1)
            def _():
                plane_rows(s, rep, True, sec).wait_send()
                each_rep(lambda source: plane_rows(s, source, False, sec).wait_send())

                def onward(slot, carry):
                    onward_rows(s, side, slot).wait_send()
                    return carry
                lax.fori_loop(0, middle, onward, 0)

    each_section(sent)
    kept_rows(rep, True).wait()
    each_rep(lambda source: kept_rows(source, False).wait())
    each_rep(lambda peer: x_copy(peer, rep).wait_send())
    each_rep(lambda peer: c_copy(peer, rep).wait_send())
    each_rep(lambda peer: g_copy(peer, rep).wait_send())
    each_rep(lambda peer: g_copy(peer, peer).wait_recv())


def window_body(inputs, cotangent, in_weight, out_weight, norm_gain, lengths):
    sections, replicas = lax.axis_size("section"), lax.axis_size("rep")
    sec, rep = lax.axis_index("section"), lax.axis_index("rep")
    micro_count, tok_rows, width = inputs.shape
    block, rank = in_weight.shape[1:]
    own_rows = micro_count * tok_rows
    chunk = own_rows // sections
    rows = chunk * replicas
    grad_scale = 1.0 / math.sqrt(own_rows * replicas)
    keep = jnp.arange(tok_rows, dtype=jnp.int32)[None, :] < lengths[0][:, None]

    def part(array):
        return lax.dynamic_slice_in_dim(array.reshape(own_rows, width), sec * chunk, chunk, 0)

    kept = lax.dynamic_slice_in_dim(keep.reshape(own_rows), sec * chunk, chunk, 0)
    x_parts = part(inputs)
    c_parts = jnp.where(kept[:, None], part(cotangent), jnp.zeros((), jnp.bfloat16))
    gain = lax.dynamic_slice_in_dim(norm_gain[0], rep * block, block, 0)[:, None]
    scaled = (in_weight[0].astype(jnp.float32) * gain).astype(jnp.bfloat16)
    bf, f32 = jnp.bfloat16, jnp.float32
    dma = pltpu.SemaphoreType.DMA
    vmem = pl.BlockSpec(memory_space=pltpu.VMEM)
    wide = rank + carrier
    stops = replicas // 2
    grad_in, grad_out, grad_gain, grad_rows = pl.pallas_call(
        functools.partial(window_kernel, sections, replicas, grad_scale),
        out_shape=(
            jax.ShapeDtypeStruct((block, rank), bf),
            jax.ShapeDtypeStruct((block, rank), bf),
            jax.ShapeDtypeStruct((8, width), f32),
            jax.ShapeDtypeStruct((own_rows, width), bf),
        ),
        in_specs=[vmem] * 6,
        out_specs=(vmem, vmem, vmem, pl.BlockSpec(memory_space=pl.ANY)),
        scratch_shapes=[
            pltpu.VMEM((sections, rows, block), bf),
            pltpu.VMEM((sections + 1, rows, block), bf),
            pltpu.VMEM((sections, block, rank), bf),
            pltpu.VMEM((sections, block, rank), bf),
            pltpu.VMEM((sections, rows, wide), bf),
            pltpu.VMEM((sections, rows // 2, wide), bf),
            pltpu.VMEM((sections, rows // 2, wide), bf),
            pltpu.VMEM((sections, stops, chunk, wide), bf),
            pltpu.VMEM((sections, rows, rank), bf),
            pltpu.VMEM((sections, rows // 2, rank), bf),
            pltpu.VMEM((sections, rows // 2, rank), bf),
            pltpu.VMEM((sections, stops, chunk, rank), bf),
            pltpu.VMEM((sections, rows, rank), bf),
            pltpu.VMEM((sections, rows, wide), bf),
            pltpu.VMEM((sections, chunk, rank), f32),
            pltpu.VMEM((sections, chunk, carrier), f32),
            *[pltpu.VMEM((sections, block, rank), bf)] * 2,
            *[pltpu.VMEM((sections, block // 2, rank), bf)] * 2,
            *[pltpu.VMEM((2, block, rank), bf)] * 2,
            pltpu.VMEM((sections, replicas, chunk, block), bf),
            pltpu.VMEM((sections, replicas // 2, chunk, block), bf),
            pltpu.VMEM((8, block), f32),
            *[dma((replicas,))] * 4,
            *[dma((sections,))] * 4,
            *[dma((sections,))] * 4,
            *[dma((sections, stops))] * 12,
            *[dma((sections, 2)), dma((sections,)), dma((sections, 2)), dma((2, 2))] * 2,
            *[dma((sections, replicas))] * 5,
            *[dma((sections, replicas // 2))] * 2,
            *[dma((replicas,))] * 3,
        ],
        compiler_params=pltpu.CompilerParams(
            collective_id=0, has_side_effects=True, vmem_limit_bytes=40 * 1024 * 1024
        ),
        name="adapter_window",
    )(x_parts, c_parts, scaled, out_weight[0], in_weight[0], gain)
    return (
        grad_in[None],
        grad_out[None],
        grad_gain[:1],
        grad_rows.reshape(1, micro_count, tok_rows, width),
    )


def body(inputs, cotangent, in_weight, out_weight, norm_gain, lengths):
    sections = lax.axis_size("section")
    block, rank = in_weight.shape[1:]
    own_rows = inputs.shape[0] * inputs.shape[1]
    aligned = own_rows % (16 * sections) == 0 and block % 128 == 0 and rank % 128 == 0
    square = sections == 4 and lax.axis_size("rep") % 2 == 0
    chosen = window_body if aligned and square else staged_body
    return chosen(inputs, cotangent, in_weight, out_weight, norm_gain, lengths)


def solution(mesh):
    in_specs = (
        P(None, "rep", None),
        P(None, "rep", None),
        P("section", "rep", None),
        P("section", "rep", None),
        P("section", None),
        P("rep", None),
    )
    out_specs = (
        P("section", "rep", None),
        P("section", "rep", None),
        P("section", None),
        P("section", None, "rep", None),
    )
    return jax.shard_map(body, mesh=mesh, in_specs=in_specs, out_specs=out_specs, check_vma=False)
```
